32 devices in a mesh: seq: 16 (over z, x, core), head: 2 (over y).
Axes of the slice: x: 2, y: 2, z: 4, core: 2. Of those that a mesh axis runs over, the one named last changes fastest.
Arguments:
- query_rows: bfloat16 [16384, 128], P('seq'), may hold values from -6 to 6
- key_rows: bfloat16 [16384, 128], P('seq'), may hold values from -6 to 6
- value_rows: bfloat16 [16384, 4096], P('seq', 'head'), may hold values from -6 to 6
- gate_rows: bfloat16 [16384, 4096], P('seq', 'head'), may hold values from -6 to 6
- norm_gain: float32 [4096], P('head'), may hold values from 0.25 to 1.75
- level_table: float32 [16], replicated, may hold values from 0.25 to 4
- level_index: int32 [32, 11], P('head'), may hold values from 0 to 15
- out_weight: bfloat16 [2048, 4096], P('seq', 'head'), may hold values from -0.09375 to 0.09375
Outputs:
- mixed_tokens: bfloat16 [16384, 2048], P('seq', 'head')
The draws below stay inside these ranges and needn't reach their ends.
All inputs are finite; a program needn't handle non-finite values.
Results may differ from the reference program's by a relative error of at most 0.014.
Values may be sent and summed in bfloat16 or wider, within the bound.
A program may use at most 128 MiB of HBM per device.

```python
import math
import jax
import jax.numpy as jnp
from jax import lax

BLOCK = 64
STATE = 128
HEAD_DIM = 128
HEADS = 32
MODEL = 2048
LEVELS = 11
TABLE = 16
TOK_DEV = 1024
TOKENS = 16384
INNER = 4096
N_SEQ = 16
N_HEAD = 2


def draw_gate_rows(key, part):
    base = jax.random.normal(key, (TOKENS, INNER), jnp.float32)
    column = jnp.arange(INNER, dtype=jnp.float32) / INNER
    scale = 0.6 * 3.0 ** column
    return jnp.clip(base * scale[None, :], -6.0, 6.0).astype(jnp.bfloat16)


def place_ends(values, stream_key, smallest, largest):
    shape = values.shape
    spot = [jax.random.randint(jax.random.fold_in(stream_key, axis), (), 0, shape[axis]) for axis in range(len(shape))]
    values = values.at[tuple(spot)].set(smallest)
    longest = shape.index(max(shape))
    spot[longest] = (spot[longest] + 1) % shape[longest]
    return values.at[tuple(spot)].set(largest)


def shard_levels(rng, shape, cuts, low, top_value):
    def one(axis_at, blocks):
        draws = jax.random.uniform(jax.random.fold_in(jax.random.fold_in(rng, 6), axis_at), (blocks,), jnp.float32, low / len(cuts), top_value / len(cuts))
        return jnp.repeat(jnp.exp(draws), shape[axis_at] // blocks).reshape((-1,) + (1,) * (len(shape) - axis_at - 1))

    gain = one(*cuts[0])
    for cut in cuts[1:]:
        gain = gain * one(*cut)
    return gain


def bell_draw(rng, shape, width, bound, split=(), kind=jnp.bfloat16):
    array = width * jax.random.normal(rng, shape, jnp.float32)
    if split:
        array = array * shard_levels(rng, shape, split, -0.22, 0.18)
    return jnp.clip(array, -bound, bound).astype(kind)


def setup_inputs(seed: int = 0) -> dict:
    keys = jax.random.split(jax.random.key(seed), 9)
    query_rows = bell_draw(keys[0], (TOKENS, STATE), 1.0, 6.0, ((0, 16),))
    key_rows = bell_draw(keys[1], (TOKENS, STATE), 1.0, 6.0, ((0, 16),))
    value_rows = bell_draw(keys[2], (TOKENS, INNER), 1.0, 6.0, ((0, 16), (1, 2)))
    gate_rows = draw_gate_rows(jax.random.fold_in(keys[8], 71), 0)
    norm_gain = jnp.clip(1.0 + 0.15 * jax.random.normal(keys[4], (INNER,), jnp.float32), 0.25, 1.75)
    level_table = jnp.clip(jnp.exp(jax.random.uniform(keys[5], (TABLE,), jnp.float32, math.log(0.25), math.log(4.0))), 0.25, 4.0)
    level_index = place_ends(jax.random.randint(keys[6], (HEADS, LEVELS), 0, TABLE), jax.random.fold_in(keys[6], 1), 0, TABLE - 1).astype(jnp.int32)
    out_weight = bell_draw(keys[7], (MODEL, INNER), INNER ** -0.5, 0.09375, ((0, 16), (1, 2)))
    return dict(query_rows=query_rows, key_rows=key_rows, value_rows=value_rows, gate_rows=gate_rows, norm_gain=norm_gain, level_table=level_table, level_index=level_index, out_weight=out_weight)


EPSILON = 1e-05

def level_weights(level_table, level_index):
    chosen = level_table[level_index]
    tiers = jnp.arange(LEVELS)
    bucket_sizes = BLOCK * jnp.exp2(jnp.maximum(tiers - 1, 0).astype(jnp.float32))
    return chosen / jnp.sqrt(bucket_sizes)

def head_mix(query_blocks, key_blocks, value_head, head_weights, causal_mask):
    query_full = query_blocks.astype(jnp.float32)
    key_full = key_blocks.astype(jnp.float32)
    value_full = value_head.astype(jnp.float32)
    scores = jnp.einsum('ctn,csn->cts', query_full, key_full)
    masked = (scores * causal_mask).astype(jnp.bfloat16)
    inside = jnp.einsum('cts,csp->ctp', masked.astype(jnp.float32), value_full)
    states = jnp.einsum('csn,csp->cnp', key_full, value_full)
    count = states.shape[0]
    combined = jnp.zeros_like(states)
    for tier_num in range(1, count.bit_length()):
        span_width = 2 ** (tier_num - 1)
        groups = count // (2 * span_width)
        shaped = states.reshape(groups, 2, span_width, states.shape[1], states.shape[2])
        lower_sum = lax.optimization_barrier(jnp.sum(shaped[:, 0], axis=1))
        placed = jnp.stack([jnp.zeros_like(lower_sum), lower_sum * head_weights[tier_num]], axis=1)
        combined = combined + jnp.broadcast_to(placed[:, :, None], shaped.shape).reshape(states.shape)
    carried = combined.astype(jnp.bfloat16)
    past_part = jnp.einsum('ctn,cnp->ctp', query_full, carried.astype(jnp.float32))
    return head_weights[0] * inside + past_part

def reference(query_rows, key_rows, value_rows, gate_rows, norm_gain, level_table, level_index, out_weight):
    count = TOKENS // BLOCK
    query_blocks = query_rows.reshape(count, BLOCK, STATE)
    key_blocks = key_rows.reshape(count, BLOCK, STATE)
    positions = jnp.arange(BLOCK)
    causal_mask = (positions[:, None] >= positions[None, :]).astype(jnp.float32)
    weights = level_weights(level_table, level_index)
    value_heads = value_rows.reshape(count, BLOCK, HEADS, HEAD_DIM).transpose(2, 0, 1, 3)

    def one_head(packed):
        value_head, head_weights = packed
        return head_mix(query_blocks, key_blocks, value_head, head_weights, causal_mask)
    mixed_heads = lax.map(one_head, (value_heads, weights)).reshape(HEADS, TOKENS, HEAD_DIM)
    group_width = INNER // N_HEAD

    def one_slab(slab_index):
        first_row = slab_index * TOK_DEV
        slab = lax.dynamic_slice_in_dim(mixed_heads, first_row, TOK_DEV, 1)
        mixed_rows = slab.transpose(1, 0, 2).reshape(TOK_DEV, INNER)
        gate_slab = lax.dynamic_slice_in_dim(gate_rows, first_row, TOK_DEV, 0)
        gated_rows = mixed_rows * jax.nn.silu(gate_slab.astype(jnp.float32))
        square_sum = lax.optimization_barrier(jnp.sum(gated_rows * gated_rows, axis=1, keepdims=True))
        normed = (gated_rows * lax.rsqrt(square_sum / INNER + EPSILON) * norm_gain).astype(jnp.bfloat16)
        total = jnp.zeros((TOK_DEV, MODEL), jnp.float32)
        for group in range(N_HEAD):
            low_col = group * group_width
            high_col = low_col + group_width
            partial_sum = jnp.dot(normed[:, low_col:high_col], out_weight[:, low_col:high_col].T, preferred_element_type=jnp.float32)
            rounded = lax.optimization_barrier(partial_sum.astype(jnp.bfloat16))
            total = total + rounded.astype(jnp.float32)
        return total.astype(jnp.bfloat16)
    slabs = lax.map(one_slab, jnp.arange(N_SEQ, dtype=jnp.int32))
    return slabs.reshape(TOKENS, MODEL)
```

```python
import functools

import jax
import jax.numpy as jnp
from jax import lax
from jax.experimental import pallas as pl
from jax.experimental.pallas import tpu as pltpu
from jax.sharding import PartitionSpec as P

BLOCK = 64
INNER = 4096
EPSILON = 1e-05
F32 = jnp.float32
BF16 = jnp.bfloat16
MESH = pl.DeviceIdType.MESH


def dot(a, b, dims):
    return lax.dot_general(a, b, (dims, ((), ())), preferred_element_type=F32)


def kernel(
    S, H, q_ref, k_ref, v_ref, gate_hbm, gain_ref, lam_ref, w_hbm, out_ref,
    gate, wbuf, loc, gbuf, gsc, tot, tb, rsib, half_f, half_b, r1, qf, qb, rq, xs, xr, hs, hr, acr,
    ssq_own, ssq_all, psend, precv, pown,
    lsem, ssem, rsem, wr, wa, wb, wc, qs, qr, ps, pr,
):
    tok, state = q_ref.shape
    cols = v_ref.shape[1]
    mr = w_hbm.shape[0]
    blocks = tok // BLOCK
    levels = blocks.bit_length() - 1
    nbits = S.bit_length() - 1
    qw = cols // 4
    A = min(4, S // 2)
    B = S // (2 * A)
    s = lax.axis_index("seq")
    h = lax.axis_index("head")
    core, b_pos, a_pos = s % 2, (s // 2) % B, s // (2 * B)

    barrier = pltpu.get_barrier_semaphore()
    for d in range(1, S):
        pl.semaphore_signal(barrier, inc=1, device_id={"seq": (s + d) % S}, device_id_type=MESH)
    for d in range(1, H):
        pl.semaphore_signal(barrier, inc=1, device_id={"head": (h + d) % H}, device_id_type=MESH)
    gate_copy = pltpu.make_async_copy(gate_hbm, gate, lsem.at[0])
    gate_copy.start()
    own_copy = pltpu.make_async_copy(w_hbm, wbuf.at[s], lsem.at[1])
    own_copy.start()

    for i in range(4):
        t = dot(k_ref[...], v_ref[:, i * qw:(i + 1) * qw], ((0,), (0,)))
        tot[i] = t
        tb[i] = t.astype(BF16)
    pl.semaphore_wait(barrier, S + H - 2)

    pending = []

    def remote(src, dst, send, recv, target):
        return pltpu.make_async_remote_copy(
            src_ref=src, dst_ref=dst, send_sem=send, recv_sem=recv,
            device_id=target, device_id_type=MESH,
        )

    def when(cond, fn):
        if cond is True:
            fn()
        else:
            pl.when(cond)(fn)

    def w_send(cond, block, own, target, sem):
        copy = remote(w_hbm if own else wbuf.at[block], wbuf.at[block], sem, wr.at[block], {"seq": target})
        when(cond, lambda: copy.start())
        pending.append((cond, copy))

    def w_wait(cond, block, sem):
        copy = remote(wbuf.at[block], wbuf.at[block], sem, wr.at[block], {"seq": s ^ 1})
        when(cond, lambda: copy.wait_recv())

    def both(x, y):
        return y if x is True else (x if y is True else jnp.logical_and(x, y))

    def blk(a, b, c):
        return (a * B + b) * 2 + c

    def clamp(x, n):
        return jnp.minimum(jnp.maximum(x, 0), n - 1)

    def send_b(cond, ab, own):
        block = blk(ab, b_pos, core)
        if B > 1:
            w_send(both(cond, b_pos < B - 1), block, own, blk(a_pos, clamp(b_pos + 1, B), core), wb.at[0, ab * B + b_pos])
            w_send(both(cond, b_pos > 0), block, own, blk(a_pos, clamp(b_pos - 1, B), core), wb.at[1, ab * B + b_pos])

    def send_core(cond, ab, bb, own):
        w_send(cond, blk(ab, bb, core), own, s ^ 1, wc.at[ab * B + bb])

    def step_a(j):
        for sign in (1, -1):
            ab = a_pos - sign * j
            cond = ab >= 0 if sign == 1 else ab <= A - 1
            ab = clamp(ab, A)
            block = blk(ab, b_pos, core)
            w_wait(cond, block, wc.at[0])
            onward = a_pos < A - 1 if sign == 1 else a_pos > 0
            nxt = clamp(a_pos + sign, A)
            w_send(both(cond, onward), block, False, blk(nxt, b_pos, core), wa.at[(1 - sign) // 2, ab])
            send_b(cond, ab, False)
            send_core(cond, ab, b_pos, False)

    def steps_b():
        for j in range(1, B):
            for sign in (1, -1):
                bb = b_pos - sign * j
                cond = bb >= 0 if sign == 1 else bb <= B - 1
                bb = clamp(bb, B)
                onward = both(cond, b_pos < B - 1 if sign == 1 else b_pos > 0)
                for i in range(A):
                    ab = lax.rem(a_pos + i, A)
                    block = blk(ab, bb, core)
                    w_wait(cond, block, wc.at[0])
                    if B > 2:
                        w_send(onward, block, False, blk(a_pos, clamp(b_pos + sign, B), core), wb.at[(1 - sign) // 2, ab * B + bb])
                    send_core(cond, ab, bb, False)

    def s_send(i, src, dst, target):
        copy = remote(src, dst, ssem.at[i], rsem.at[i], {"seq": target})
        copy.start()
        return copy

    tw = min(256, cols)
    tiles = cols // tw

    def local_tiles(lo, hi):
        @pl.loop(lo, hi)
        def _(ct):
            at = pl.ds(pl.multiple_of(ct * tw, tw), tw)
            lam = lam_ref[:, at]

            def vals(c):
                return v_ref[pl.ds(c * BLOCK, BLOCK), at]

            def total(lo_c, n):
                if n == 1:
                    r = pl.ds(lo_c * BLOCK, BLOCK)
                    return dot(k_ref[r, :], vals(lo_c), ((0,), (0,)))
                return sums[(lo_c, n // 2)] + sums[(lo_c + n // 2, n // 2)]

            sums = {}
            n = 1
            while n < blocks:
                for lo_c in range(0, blocks, n):
                    sums[(lo_c, n)] = total(lo_c, n)
                n *= 2

            def walk(lo_c, n, base):
                if n == 1:
                    r = pl.ds(lo_c * BLOCK, BLOCK)
                    m = lam[0:1] * dot(gsc[lo_c], vals(lo_c), ((1,), (0,)))
                    if base is not None:
                        m = m + dot(q_ref[r, :], base.astype(BF16), ((1,), (0,)))
                    loc[r, at] = m
                    return
                level = n.bit_length() - 1
                add = lam[level:level + 1] * sums[(lo_c, n // 2)]
                walk(lo_c, n // 2, base)
                walk(lo_c + n // 2, n // 2, add if base is None else base + add)

            walk(0, blocks, None)

    def lam_at(level, quarter):
        return lam_ref[level:level + 1, pl.ds(pl.multiple_of(quarter * qw, qw), qw)]

    def bit(b):
        return (s >> b & 1).astype(F32)

    c0 = s_send(0, tb, rsib, s ^ 1)
    w_send(a_pos < A - 1, s, True, blk(clamp(a_pos + 1, A), b_pos, core), wa.at[0, a_pos])
    w_send(a_pos > 0, s, True, blk(clamp(a_pos - 1, A), b_pos, core), wa.at[1, a_pos])
    row = lax.broadcasted_iota(jnp.int32, (BLOCK, BLOCK), 0)
    col = lax.broadcasted_iota(jnp.int32, (BLOCK, BLOCK), 1)
    for c in range(blocks):
        r = pl.ds(c * BLOCK, BLOCK)
        scores = dot(q_ref[r, :], k_ref[r, :], ((1,), (1,)))
        gsc[c] = jnp.where(row >= col, scores, 0.0).astype(BF16)
    c0.wait()
    first = 2 * core
    for i in range(2):
        t = tot[first + i] + rsib[first + i].astype(F32)
        half_f[i] = t
        half_b[i] = t.astype(BF16)
    c1 = s_send(1, half_b, r1, s ^ 2)
    cut = [tiles * i // (nbits - 1) for i in range(nbits)]
    local_tiles(cut[0], cut[1])
    c1.wait()
    mine = s >> 1 & 1
    send_b(True, a_pos, True)
    qf[...] = half_f[mine] + r1[mine].astype(F32)
    for i in range(2):
        half_f[i] = bit(1) * lam_at(levels + 2, first + i) * r1[i].astype(F32)
    for b in range(2, nbits):
        qb[b - 2] = qf[...].astype(BF16)
        cb = s_send(b, qb.at[b - 2], rq.at[b - 2], s ^ (1 << b))
        if b == 2:
            send_core(True, a_pos, b_pos, True)
        local_tiles(cut[b - 1], cut[b])
        cb.wait()
        got = rq[b - 2].astype(F32)
        half_f[mine] += bit(b) * lam_at(levels + 1 + b, first + mine) * got
        contrib = bit(b) * lam_at(levels + 1 + b, first + mine) * got
        if b == 2:
            xs[1] = contrib
        else:
            xs[1] += contrib
        qf[...] += got
        if b == 2:
            step_a(1)
    qb[nbits - 2] = xs[1].astype(BF16)
    cx = s_send(nbits, qb.at[nbits - 2], xr, s ^ 2)
    cx.wait()
    half_f[1 - mine] += xr[...].astype(F32)
    hs[...] = half_f[...].astype(BF16)
    ch = s_send(nbits + 1, hs, hr, s ^ 1)
    for j in range(2, A):
        if j == 2:
            step_a(j)
    ch.wait()
    other = 2 - first
    for i in range(2):
        acr[first + i] = (half_f[i] + bit(0) * lam_at(levels + 1, first + i) * rsib[first + i].astype(F32)).astype(BF16)
        acr[other + i] = (
            hr[i].astype(F32) + bit(0) * lam_at(levels + 1, other + i) * rsib[other + i].astype(F32)
        ).astype(BF16)
    gate_copy.wait()

    rt = 128
    row_tiles = tok // rt

    @pl.loop(0, row_tiles)
    def _(t):
        r = pl.ds(pl.multiple_of(t * rt, rt), rt)
        squares = jnp.zeros((rt, 1), F32)
        for i in range(4):
            at = slice(i * qw, (i + 1) * qw)
            mixed = loc[r, at] + dot(q_ref[r, :], acr[i], ((1,), (0,)))
            g = gate[r, at].astype(F32)
            gated = mixed * (g / (1.0 + jnp.exp(-g)))
            squares = squares + jnp.sum(gated * gated, axis=1, keepdims=True)
            gbuf[r, at] = (gated * gain_ref[:, at]).astype(BF16)
        wide = jnp.broadcast_to(squares, (rt, 128)).T
        ssq_own[:, r] = wide[0:8]

    sq = []
    for d in range(1, H):
        copy = remote(ssq_own, ssq_all.at[d], qs.at[d], qr.at[d], {"head": (h + d) % H})
        copy.start()
        sq.append(copy)

    for j in range(3, A):
        step_a(j)
    steps_b()
    for i in range(A * B):
        w_wait(True, blk(i // B, i % B, 1 - core), wc.at[0])
    own_copy.wait()

    nj, nw = psend.shape[1], psend.shape[3]
    per = nw // mr
    pt = 256
    ptiles = tok // pt

    def product(head, j, t):
        first_block = head * (nj * per) + j * per
        w = wbuf[pl.ds(first_block, per)].reshape(nw, cols)
        r = pl.ds(pl.multiple_of(t * pt, pt), pt)
        return dot(gbuf[r, :], w, ((1,), (1,))).astype(BF16), r

    def p_copy(d, j, t):
        r = pl.ds(pl.multiple_of(t * pt, pt), pt)
        return remote(
            psend.at[d, j, r], precv.at[d, j, r], ps.at[d, j, t], pr.at[d, j, t], {"head": (h + d) % H}
        )

    for d in range(1, H):
        @pl.loop(0, nj * ptiles)
        def _(i):
            j, t = i // ptiles, i % ptiles
            val, r = product((h + d) % H, j, t)
            psend[d, j, r] = val
            p_copy(d, j, t).start()

    @pl.loop(0, nj * ptiles)
    def _(i):
        j, t = i // ptiles, i % ptiles
        val, r = product(h, j, t)
        pown[j, r] = val

    for copy in sq:
        copy.wait()

    @pl.loop(0, ptiles)
    def _(t):
        r = pl.ds(pl.multiple_of(t * pt, pt), pt)
        total = ssq_own[:, r]
        for d in range(1, H):
            total = total + ssq_all[d, :, r]
        wide = jnp.broadcast_to(total[0:1], (128, pt)).T
        loc[r, 0:128] = lax.rsqrt(wide / INNER + EPSILON)

    for j in range(nj):
        @pl.loop(0, ptiles)
        def _(t):
            r = pl.ds(pl.multiple_of(t * pt, pt), pt)
            acc = pown[j, r].astype(F32)
            for d in range(1, H):
                p_copy(d, j, t).wait_recv()
                acc = acc + precv[d, j, r].astype(F32)
            scale = loc[r, 0:128][:, 0:1]
            out_ref[r, j * nw:(j + 1) * nw] = (acc * scale).astype(BF16)

    for d in range(1, H):
        @pl.loop(0, nj * ptiles)
        def _(i):
            p_copy(d, i // ptiles, i % ptiles).wait_send()
    for cond, copy in pending:
        when(cond, lambda: copy.wait_send())


def body(query_rows, key_rows, value_rows, gate_rows, norm_gain, level_table, level_index, out_weight):
    S, H = lax.axis_size("seq"), lax.axis_size("head")
    tok, state = query_rows.shape
    cols = value_rows.shape[1]
    mr = out_weight.shape[0]
    head_width = cols // level_index.shape[0]
    nlev = level_index.shape[1]
    blocks = tok // BLOCK
    nbits = S.bit_length() - 1
    choose = (level_index[:, :, None] == jnp.arange(level_table.shape[0], dtype=jnp.int32)).astype(F32)
    picked = jnp.sum(choose * level_table, axis=2)
    tiers = jnp.arange(nlev)
    bucket_sizes = BLOCK * jnp.exp2(jnp.maximum(tiers - 1, 0).astype(F32))
    weights = picked / jnp.sqrt(bucket_sizes)
    lam = jnp.repeat(weights, head_width, axis=0).T
    model_here = mr * S // H
    nw = min(512, model_here)
    nj = model_here // nw
    qw = cols // 4
    A = min(4, S // 2)
    B = S // (2 * A)
    ptiles = tok // 256
    vm = pl.BlockSpec(memory_space=pltpu.VMEM)
    hbm = pl.BlockSpec(memory_space=pl.ANY)
    dma = pltpu.SemaphoreType.DMA
    return pl.pallas_call(
        functools.partial(kernel, S, H),
        out_shape=jax.ShapeDtypeStruct((tok, model_here), BF16),
        in_specs=[vm, vm, vm, hbm, vm, vm, hbm],
        out_specs=vm,
        scratch_shapes=[
            pltpu.VMEM((tok, cols), BF16),
            pltpu.VMEM((S, mr, cols), BF16),
            pltpu.VMEM((tok, cols), F32),
            pltpu.VMEM((tok, cols), BF16),
            pltpu.VMEM((blocks, BLOCK, BLOCK), BF16),
            pltpu.VMEM((4, state, qw), F32),
            pltpu.VMEM((4, state, qw), BF16),
            pltpu.VMEM((4, state, qw), BF16),
            pltpu.VMEM((2, state, qw), F32),
            pltpu.VMEM((2, state, qw), BF16),
            pltpu.VMEM((2, state, qw), BF16),
            pltpu.VMEM((state, qw), F32),
            pltpu.VMEM((nbits, state, qw), BF16),
            pltpu.VMEM((nbits, state, qw), BF16),
            pltpu.VMEM((2, state, qw), F32),
            pltpu.VMEM((state, qw), BF16),
            pltpu.VMEM((2, state, qw), BF16),
            pltpu.VMEM((2, state, qw), BF16),
            pltpu.VMEM((4, state, qw), BF16),
            pltpu.VMEM((8, tok), F32),
            pltpu.VMEM((H, 8, tok), F32),
            pltpu.VMEM((H, nj, tok, nw), BF16),
            pltpu.VMEM((H, nj, tok, nw), BF16),
            pltpu.VMEM((nj, tok, nw), BF16),
            dma((2,)),
            dma((nbits + 2,)),
            dma((nbits + 2,)),
            dma((S,)),
            dma((2, A)),
            dma((2, A * B)),
            dma((A * B,)),
            dma((H,)),
            dma((H,)),
            dma((H, nj, ptiles)),
            dma((H, nj, ptiles)),
        ],
        compiler_params=pltpu.CompilerParams(
            collective_id=0, has_side_effects=True, vmem_limit_bytes=66 * 2**20 - 3 * 2**20
        ),
    )(query_rows, key_rows, value_rows, gate_rows, norm_gain.reshape(1, cols), lam, out_weight)


def solution(mesh):
    in_specs = (
        P("seq", None),
        P("seq", None),
        P("seq", "head"),
        P("seq", "head"),
        P("head"),
        P(),
        P("head", None),
        P("seq", "head"),
    )
    return jax.shard_map(body, mesh=mesh, in_specs=in_specs, out_specs=P("seq", "head"), check_vma=False)
```

```python
import functools

import jax
import jax.numpy as jnp
from jax import lax
from jax.experimental import pallas as pl
from jax.experimental.pallas import tpu as pltpu
from jax.sharding import PartitionSpec as P

BLOCK = 64
INNER = 4096
EPSILON = 1e-05
F32 = jnp.float32
BF16 = jnp.bfloat16
MESH = pl.DeviceIdType.MESH


def dot(a, b, dims):
    return lax.dot_general(a, b, (dims, ((), ())), preferred_element_type=F32)


def kernel(
    S, H, q_ref, k_ref, v_ref, gate_hbm, gain_ref, lam_ref, w_hbm, out_ref,
    gate, wbuf, loc, gbuf, gsc, tot, tb, rsib, half_f, half_b, r1, qf, qb, rq, xs, xr, hs, hr, acr,
    ssq_own, ssq_all, psend, precv, pown,
    lsem, ssem, rsem, wr, wa, wb, wc, qs, qr, ps, pr,
):
    tok, state = q_ref.shape
    cols = v_ref.shape[1]
    mr = w_hbm.shape[0]
    blocks = tok // BLOCK
    levels = blocks.bit_length() - 1
    nbits = S.bit_length() - 1
    qw = cols // 4
    A = min(4, S // 2)
    B = S // (2 * A)
    s = lax.axis_index("seq")
    h = lax.axis_index("head")
    core, b_pos, a_pos = s % 2, (s // 2) % B, s // (2 * B)

    barrier = pltpu.get_barrier_semaphore()
    for d in range(1, S):
        pl.semaphore_signal(barrier, inc=1, device_id={"seq": (s + d) % S}, device_id_type=MESH)
    for d in range(1, H):
        pl.semaphore_signal(barrier, inc=1, device_id={"head": (h + d) % H}, device_id_type=MESH)
    gate_copy = pltpu.make_async_copy(gate_hbm, gate, lsem.at[0])
    gate_copy.start()
    own_copy = pltpu.make_async_copy(w_hbm, wbuf.at[s], lsem.at[1])
    own_copy.start()

    for i in range(4):
        t = dot(k_ref[...], v_ref[:, i * qw:(i + 1) * qw], ((0,), (0,)))
        tot[i] = t
        tb[i] = t.astype(BF16)
    pl.semaphore_wait(barrier, S + H - 2)

    pending = []

    def remote(src, dst, send, recv, target):
        return pltpu.make_async_remote_copy(
            src_ref=src, dst_ref=dst, send_sem=send, recv_sem=recv,
            device_id=target, device_id_type=MESH,
        )

    def when(cond, fn):
        if cond is True:
            fn()
        else:
            pl.when(cond)(fn)

    def w_send(cond, block, own, target, sem):
        copy = remote(w_hbm if own else wbuf.at[block], wbuf.at[block], sem, wr.at[block], {"seq": target})
        when(cond, lambda: copy.start())
        pending.append((cond, copy))

    def w_wait(cond, block, sem):
        copy = remote(wbuf.at[block], wbuf.at[block], sem, wr.at[block], {"seq": s ^ 1})
        when(cond, lambda: copy.wait_recv())

    def both(x, y):
        return y if x is True else (x if y is True else jnp.logical_and(x, y))

    def blk(a, b, c):
        return (a * B + b) * 2 + c

    def clamp(x, n):
        return jnp.minimum(jnp.maximum(x, 0), n - 1)

    def send_b(cond, ab, own):
        block = blk(ab, b_pos, core)
        if B > 1:
            w_send(both(cond, b_pos < B - 1), block, own, blk(a_pos, clamp(b_pos + 1, B), core), wb.at[0, ab * B + b_pos])
            w_send(both(cond, b_pos > 0), block, own, blk(a_pos, clamp(b_pos - 1, B), core), wb.at[1, ab * B + b_pos])

    def send_core(cond, ab, bb, own):
        w_send(cond, blk(ab, bb, core), own, s ^ 1, wc.at[ab * B + bb])

    def urgent(ab):
        return ab * H // A != h

    def source_a(j, sign):
        ab = a_pos - sign * j
        cond = ab >= 0 if sign == 1 else ab <= A - 1
        return cond, clamp(ab, A)

    def across_b(j, first):
        if j == 0:
            send_b(urgent(a_pos) if first else jnp.logical_not(urgent(a_pos)), a_pos, True)
            return
        for sign in (1, -1):
            cond, ab = source_a(j, sign)
            send_b(both(cond, urgent(ab) if first else jnp.logical_not(urgent(ab))), ab, False)

    def step_a(j):
        for sign in (1, -1):
            cond, ab = source_a(j, sign)
            block = blk(ab, b_pos, core)
            w_wait(cond, block, wc.at[0])
            onward = a_pos < A - 1 if sign == 1 else a_pos > 0
            nxt = clamp(a_pos + sign, A)
            w_send(both(cond, onward), block, False, blk(nxt, b_pos, core), wa.at[(1 - sign) // 2, ab])
            send_core(cond, ab, b_pos, False)

    def finish(ab):
        for j in range(1, B):
            for sign in (1, -1):
                bb = b_pos - sign * j
                cond = bb >= 0 if sign == 1 else bb <= B - 1
                bb = clamp(bb, B)
                onward = both(cond, b_pos < B - 1 if sign == 1 else b_pos > 0)
                block = blk(ab, bb, core)
                w_wait(cond, block, wc.at[0])
                if B > 2:
                    w_send(onward, block, False, blk(a_pos, clamp(b_pos + sign, B), core), wb.at[(1 - sign) // 2, ab * B + bb])
                send_core(cond, ab, bb, False)
        for bb in range(B):
            w_wait(True, blk(ab, bb, 1 - core), wc.at[0])

    def s_send(i, src, dst, target):
        copy = remote(src, dst, ssem.at[i], rsem.at[i], {"seq": target})
        copy.start()
        return copy

    tw = min(256, cols)
    tiles = cols // tw

    def local_tiles(lo, hi):
        @pl.loop(lo, hi)
        def _(ct):
            at = pl.ds(pl.multiple_of(ct * tw, tw), tw)
            lam = lam_ref[:, at]

            def vals(c):
                return v_ref[pl.ds(c * BLOCK, BLOCK), at]

            def total(lo_c, n):
                if n == 1:
                    r = pl.ds(lo_c * BLOCK, BLOCK)
                    return dot(k_ref[r, :], vals(lo_c), ((0,), (0,)))
                return sums[(lo_c, n // 2)] + sums[(lo_c + n // 2, n // 2)]

            sums = {}
            n = 1
            while n < blocks:
                for lo_c in range(0, blocks, n):
                    sums[(lo_c, n)] = total(lo_c, n)
                n *= 2

            def walk(lo_c, n, base):
                if n == 1:
                    r = pl.ds(lo_c * BLOCK, BLOCK)
                    m = lam[0:1] * dot(gsc[lo_c], vals(lo_c), ((1,), (0,)))
                    if base is not None:
                        m = m + dot(q_ref[r, :], base.astype(BF16), ((1,), (0,)))
                    loc[r, at] = m
                    return
                level = n.bit_length() - 1
                add = lam[level:level + 1] * sums[(lo_c, n // 2)]
                walk(lo_c, n // 2, base)
                walk(lo_c + n // 2, n // 2, add if base is None else base + add)

            walk(0, blocks, None)

    def lam_at(level, quarter):
        return lam_ref[level:level + 1, pl.ds(pl.multiple_of(quarter * qw, qw), qw)]

    def bit(b):
        return (s >> b & 1).astype(F32)

    c0 = s_send(0, tb, rsib, s ^ 1)
    w_send(a_pos < A - 1, s, True, blk(clamp(a_pos + 1, A), b_pos, core), wa.at[0, a_pos])
    w_send(a_pos > 0, s, True, blk(clamp(a_pos - 1, A), b_pos, core), wa.at[1, a_pos])
    row = lax.broadcasted_iota(jnp.int32, (BLOCK, BLOCK), 0)
    col = lax.broadcasted_iota(jnp.int32, (BLOCK, BLOCK), 1)
    for c in range(blocks):
        r = pl.ds(c * BLOCK, BLOCK)
        scores = dot(q_ref[r, :], k_ref[r, :], ((1,), (1,)))
        gsc[c] = jnp.where(row >= col, scores, 0.0).astype(BF16)
    c0.wait()
    first = 2 * core
    for i in range(2):
        t = tot[first + i] + rsib[first + i].astype(F32)
        half_f[i] = t
        half_b[i] = t.astype(BF16)
    c1 = s_send(1, half_b, r1, s ^ 2)
    across_b(0, True)
    send_core(True, a_pos, b_pos, True)
    cut = [tiles * i // (nbits - 1) for i in range(nbits)]
    local_tiles(cut[0], cut[1])
    c1.wait()
    mine = s >> 1 & 1
    qf[...] = half_f[mine] + r1[mine].astype(F32)
    for i in range(2):
        half_f[i] = bit(1) * lam_at(levels + 2, first + i) * r1[i].astype(F32)
    for b in range(2, nbits):
        qb[b - 2] = qf[...].astype(BF16)
        cb = s_send(b, qb.at[b - 2], rq.at[b - 2], s ^ (1 << b))
        local_tiles(cut[b - 1], cut[b])
        if b == nbits - 1:
            step_a(1)
        cb.wait()
        got = rq[b - 2].astype(F32)
        half_f[mine] += bit(b) * lam_at(levels + 1 + b, first + mine) * got
        contrib = bit(b) * lam_at(levels + 1 + b, first + mine) * got
        if b == 2:
            xs[1] = contrib
        else:
            xs[1] += contrib
        qf[...] += got
    qb[nbits - 2] = xs[1].astype(BF16)
    cx = s_send(nbits, qb.at[nbits - 2], xr, s ^ 2)
    across_b(1, True)
    cx.wait()
    half_f[1 - mine] += xr[...].astype(F32)
    hs[...] = half_f[...].astype(BF16)
    ch = s_send(nbits + 1, hs, hr, s ^ 1)
    ch.wait()
    other = 2 - first
    for i in range(2):
        acr[first + i] = (half_f[i] + bit(0) * lam_at(levels + 1, first + i) * rsib[first + i].astype(F32)).astype(BF16)
        acr[other + i] = (
            hr[i].astype(F32) + bit(0) * lam_at(levels + 1, other + i) * rsib[other + i].astype(F32)
        ).astype(BF16)
    gate_copy.wait()
    for j in range(2, min(3, A)):
        step_a(j)
        across_b(j, True)

    rt = 128
    row_tiles = tok // rt

    @pl.loop(0, row_tiles)
    def _(t):
        r = pl.ds(pl.multiple_of(t * rt, rt), rt)
        squares = jnp.zeros((rt, 1), F32)
        for i in range(4):
            at = slice(i * qw, (i + 1) * qw)
            mixed = loc[r, at] + dot(q_ref[r, :], acr[i], ((1,), (0,)))
            g = gate[r, at].astype(F32)
            gated = mixed * (g / (1.0 + jnp.exp(-g)))
            squares = squares + jnp.sum(gated * gated, axis=1, keepdims=True)
            gbuf[r, at] = (gated * gain_ref[:, at]).astype(BF16)
        wide = jnp.broadcast_to(squares, (rt, 128)).T
        ssq_own[:, r] = wide[0:8]

    sq = []
    for d in range(1, H):
        copy = remote(ssq_own, ssq_all.at[d], qs.at[d], qr.at[d], {"head": (h + d) % H})
        copy.start()
        sq.append(copy)

    own_copy.wait()

    nj, nw = psend.shape[1], psend.shape[3]
    per = nw // mr
    pt = 256
    ptiles = tok // pt

    def product(head, j, t):
        first_block = head * (nj * per) + j * per
        w = wbuf[pl.ds(first_block, per)].reshape(nw, cols)
        r = pl.ds(pl.multiple_of(t * pt, pt), pt)
        return dot(gbuf[r, :], w, ((1,), (1,))).astype(BF16), r

    def p_copy(d, j, t):
        r = pl.ds(pl.multiple_of(t * pt, pt), pt)
        return remote(
            psend.at[d, j, r], precv.at[d, j, r], ps.at[d, j, t], pr.at[d, j, t], {"head": (h + d) % H}
        )

    def far_steps():
        for j in range(3, A):
            step_a(j)
            across_b(j, True)
        for j in range(A):
            across_b(j, False)

    def send_chunk(d, j):
        @pl.loop(0, ptiles)
        def _(t):
            val, r = product((h + d) % H, j, t)
            psend[d, j, r] = val
            p_copy(d, j, t).start()

    def own_chunk(j):
        @pl.loop(0, ptiles)
        def _(t):
            val, r = product(h, j, t)
            pown[j, r] = val

    one_row = H == 2 and nj * H == A
    order = list(range(nj))
    if one_row:
        low = (1 - h) * nj
        near = jnp.where(jnp.abs(low - a_pos) <= jnp.abs(low + 1 - a_pos), 0, 1)
        order = [near, 1 - near]
        for i, j in enumerate(order):
            if i == 1:
                far_steps()
            finish(low + j)
            send_chunk(1, j)
        for j in range(nj):
            finish(h * nj + j)
            own_chunk(j)
    else:
        far_steps()
        for i in range(A):
            finish(i)
        for d in range(1, H):
            for j in range(nj):
                send_chunk(d, j)
        for j in range(nj):
            own_chunk(j)

    for copy in sq:
        copy.wait()

    @pl.loop(0, ptiles)
    def _(t):
        r = pl.ds(pl.multiple_of(t * pt, pt), pt)
        total = ssq_own[:, r]
        for d in range(1, H):
            total = total + ssq_all[d, :, r]
        wide = jnp.broadcast_to(total[0:1], (128, pt)).T
        loc[r, 0:128] = lax.rsqrt(wide / INNER + EPSILON)

    for j in range(nj):
        @pl.loop(0, ptiles)
        def _(t, j=j):
            r = pl.ds(pl.multiple_of(t * pt, pt), pt)
            acc = pown[j, r].astype(F32)
            for d in range(1, H):
                p_copy(d, j, t).wait_recv()
                acc = acc + precv[d, j, r].astype(F32)
            scale = loc[r, 0:128][:, 0:1]
            out_ref[r, j * nw:(j + 1) * nw] = (acc * scale).astype(BF16)

    for d in range(1, H):
        @pl.loop(0, nj * ptiles)
        def _(i):
            p_copy(d, i // ptiles, i % ptiles).wait_send()
    for cond, copy in pending:
        when(cond, lambda: copy.wait_send())


def body(query_rows, key_rows, value_rows, gate_rows, norm_gain, level_table, level_index, out_weight):
    S, H = lax.axis_size("seq"), lax.axis_size("head")
    tok, state = query_rows.shape
    cols = value_rows.shape[1]
    mr = out_weight.shape[0]
    head_width = cols // level_index.shape[0]
    nlev = level_index.shape[1]
    blocks = tok // BLOCK
    nbits = S.bit_length() - 1
    choose = (level_index[:, :, None] == jnp.arange(level_table.shape[0], dtype=jnp.int32)).astype(F32)
    picked = jnp.sum(choose * level_table, axis=2)
    tiers = jnp.arange(nlev)
    bucket_sizes = BLOCK * jnp.exp2(jnp.maximum(tiers - 1, 0).astype(F32))
    weights = picked / jnp.sqrt(bucket_sizes)
    lam = jnp.repeat(weights, head_width, axis=0).T
    model_here = mr * S // H
    nw = min(512, model_here)
    nj = model_here // nw
    qw = cols // 4
    A = min(4, S // 2)
    B = S // (2 * A)
    ptiles = tok // 256
    vm = pl.BlockSpec(memory_space=pltpu.VMEM)
    hbm = pl.BlockSpec(memory_space=pl.ANY)
    dma = pltpu.SemaphoreType.DMA
    return pl.pallas_call(
        functools.partial(kernel, S, H),
        out_shape=jax.ShapeDtypeStruct((tok, model_here), BF16),
        in_specs=[vm, vm, vm, hbm, vm, vm, hbm],
        out_specs=vm,
        scratch_shapes=[
            pltpu.VMEM((tok, cols), BF16),
            pltpu.VMEM((S, mr, cols), BF16),
            pltpu.VMEM((tok, cols), F32),
            pltpu.VMEM((tok, cols), BF16),
            pltpu.VMEM((blocks, BLOCK, BLOCK), BF16),
            pltpu.VMEM((4, state, qw), F32),
            pltpu.VMEM((4, state, qw), BF16),
            pltpu.VMEM((4, state, qw), BF16),
            pltpu.VMEM((2, state, qw), F32),
            pltpu.VMEM((2, state, qw), BF16),
            pltpu.VMEM((2, state, qw), BF16),
            pltpu.VMEM((state, qw), F32),
            pltpu.VMEM((nbits, state, qw), BF16),
            pltpu.VMEM((nbits, state, qw), BF16),
            pltpu.VMEM((2, state, qw), F32),
            pltpu.VMEM((state, qw), BF16),
            pltpu.VMEM((2, state, qw), BF16),
            pltpu.VMEM((2, state, qw), BF16),
            pltpu.VMEM((4, state, qw), BF16),
            pltpu.VMEM((8, tok), F32),
            pltpu.VMEM((H, 8, tok), F32),
            pltpu.VMEM((H, nj, tok, nw), BF16),
            pltpu.VMEM((H, nj, tok, nw), BF16),
            pltpu.VMEM((nj, tok, nw), BF16),
            dma((2,)),
            dma((nbits + 2,)),
            dma((nbits + 2,)),
            dma((S,)),
            dma((2, A)),
            dma((2, A * B)),
            dma((A * B,)),
            dma((H,)),
            dma((H,)),
            dma((H, nj, ptiles)),
            dma((H, nj, ptiles)),
        ],
        compiler_params=pltpu.CompilerParams(
            collective_id=0, has_side_effects=True, vmem_limit_bytes=66 * 2**20 - 3 * 2**20
        ),
    )(query_rows, key_rows, value_rows, gate_rows, norm_gain.reshape(1, cols), lam, out_weight)


def solution(mesh):
    in_specs = (
        P("seq", None),
        P("seq", None),
        P("seq", "head"),
        P("seq", "head"),
        P("head"),
        P(),
        P("head", None),
        P("seq", "head"),
    )
    return jax.shard_map(body, mesh=mesh, in_specs=in_specs, out_specs=P("seq", "head"), check_vma=False)
```

```python
import functools

import jax
import jax.numpy as jnp
from jax import lax
from jax.experimental import pallas as pl
from jax.experimental.pallas import tpu as pltpu
from jax.sharding import PartitionSpec as P

BLOCK = 64
INNER = 4096
EPSILON = 1e-05
F32 = jnp.float32
BF16 = jnp.bfloat16
MESH = pl.DeviceIdType.MESH


def dot(a, b, dims):
    return lax.dot_general(a, b, (dims, ((), ())), preferred_element_type=F32)


def kernel(
    S, H, q_ref, k_ref, v_ref, gate_hbm, gain_ref, lam_ref, w_hbm, out_ref,
    gate, wbuf, loc, gbuf, gsc, tot, tb, rsib, half_f, half_b, r1, qf, qb, rq, xs, xr, hs, hr, acr,
    ssq_own, ssq_all, psend, precv, pown,
    lsem, ssem, rsem, wr, wa, wb, wc, qs, qr, ps, pr,
):
    tok, state = q_ref.shape
    cols = v_ref.shape[1]
    mr = w_hbm.shape[0]
    blocks = tok // BLOCK
    levels = blocks.bit_length() - 1
    nbits = S.bit_length() - 1
    qw = cols // 4
    A = min(4, S // 2)
    B = S // (2 * A)
    s = lax.axis_index("seq")
    h = lax.axis_index("head")
    core, b_pos, a_pos = s % 2, (s // 2) % B, s // (2 * B)

    barrier = pltpu.get_barrier_semaphore()
    for d in range(1, S):
        pl.semaphore_signal(barrier, inc=1, device_id={"seq": (s + d) % S}, device_id_type=MESH)
    for d in range(1, H):
        pl.semaphore_signal(barrier, inc=1, device_id={"head": (h + d) % H}, device_id_type=MESH)
    gate_copy = pltpu.make_async_copy(gate_hbm, gate, lsem.at[0])
    gate_copy.start()
    own_copy = pltpu.make_async_copy(w_hbm, wbuf.at[s], lsem.at[1])
    own_copy.start()

    for i in range(4):
        t = dot(k_ref[...], v_ref[:, i * qw:(i + 1) * qw], ((0,), (0,)))
        tot[i] = t
        tb[i] = t.astype(BF16)
    pl.semaphore_wait(barrier, S + H - 2)

    pending = []

    def remote(src, dst, send, recv, target):
        return pltpu.make_async_remote_copy(
            src_ref=src, dst_ref=dst, send_sem=send, recv_sem=recv,
            device_id=target, device_id_type=MESH,
        )

    def when(cond, fn):
        if cond is True:
            fn()
        else:
            pl.when(cond)(fn)

    def w_send(cond, block, own, target, sem):
        copy = remote(w_hbm if own else wbuf.at[block], wbuf.at[block], sem, wr.at[block], {"seq": target})
        when(cond, lambda: copy.start())
        pending.append((cond, copy))

    def w_wait(cond, block, sem):
        copy = remote(wbuf.at[block], wbuf.at[block], sem, wr.at[block], {"seq": s ^ 1})
        when(cond, lambda: copy.wait_recv())

    def both(x, y):
        return y if x is True else (x if y is True else jnp.logical_and(x, y))

    def blk(a, b, c):
        return (a * B + b) * 2 + c

    def clamp(x, n):
        return jnp.minimum(jnp.maximum(x, 0), n - 1)

    def send_b(cond, ab, own):
        block = blk(ab, b_pos, core)
        if B > 1:
            w_send(both(cond, b_pos < B - 1), block, own, blk(a_pos, clamp(b_pos + 1, B), core), wb.at[0, ab * B + b_pos])
            w_send(both(cond, b_pos > 0), block, own, blk(a_pos, clamp(b_pos - 1, B), core), wb.at[1, ab * B + b_pos])

    def send_core(cond, ab, bb, own):
        w_send(cond, blk(ab, bb, core), own, s ^ 1, wc.at[ab * B + bb])

    def urgent(ab):
        return ab * H // A != h

    def source_a(j, sign):
        ab = a_pos - sign * j
        cond = ab >= 0 if sign == 1 else ab <= A - 1
        return cond, clamp(ab, A)

    def across_b(j, first):
        if j == 0:
            send_b(True, a_pos, True)
            return
        for sign in (1, -1):
            cond, ab = source_a(j, sign)
            send_b(both(cond, urgent(ab) if first else jnp.logical_not(urgent(ab))), ab, False)

    def step_a(j):
        for sign in (1, -1):
            cond, ab = source_a(j, sign)
            block = blk(ab, b_pos, core)
            w_wait(cond, block, wc.at[0])
            onward = a_pos < A - 1 if sign == 1 else a_pos > 0
            nxt = clamp(a_pos + sign, A)
            w_send(both(cond, onward), block, False, blk(nxt, b_pos, core), wa.at[(1 - sign) // 2, ab])
            send_core(cond, ab, b_pos, False)

    def finish_own(ab):
        w_wait(True, blk(ab, b_pos, 1 - core), wc.at[0])

    def finish_rest(ab):
        for j in range(1, B):
            for sign in (1, -1):
                bb = b_pos - sign * j
                cond = bb >= 0 if sign == 1 else bb <= B - 1
                bb = clamp(bb, B)
                onward = both(cond, b_pos < B - 1 if sign == 1 else b_pos > 0)
                block = blk(ab, bb, core)
                w_wait(cond, block, wc.at[0])
                if B > 2:
                    w_send(onward, block, False, blk(a_pos, clamp(b_pos + sign, B), core), wb.at[(1 - sign) // 2, ab * B + bb])
                send_core(cond, ab, bb, False)
        for j in range(1, B):
            w_wait(True, blk(ab, lax.rem(b_pos + j, B), 1 - core), wc.at[0])

    def s_send(i, src, dst, target):
        copy = remote(src, dst, ssem.at[i], rsem.at[i], {"seq": target})
        copy.start()
        return copy

    tw = min(256, cols)
    tiles = cols // tw

    def local_tiles(lo, hi):
        @pl.loop(lo, hi)
        def _(ct):
            at = pl.ds(pl.multiple_of(ct * tw, tw), tw)
            lam = lam_ref[:, at]

            def vals(c):
                return v_ref[pl.ds(c * BLOCK, BLOCK), at]

            def total(lo_c, n):
                if n == 1:
                    r = pl.ds(lo_c * BLOCK, BLOCK)
                    return dot(k_ref[r, :], vals(lo_c), ((0,), (0,)))
                return sums[(lo_c, n // 2)] + sums[(lo_c + n // 2, n // 2)]

            sums = {}
            n = 1
            while n < blocks:
                for lo_c in range(0, blocks, n):
                    sums[(lo_c, n)] = total(lo_c, n)
                n *= 2

            def walk(lo_c, n, base):
                if n == 1:
                    r = pl.ds(lo_c * BLOCK, BLOCK)
                    m = lam[0:1] * dot(gsc[lo_c], vals(lo_c), ((1,), (0,)))
                    if base is not None:
                        m = m + dot(q_ref[r, :], base.astype(BF16), ((1,), (0,)))
                    loc[r, at] = m
                    return
                level = n.bit_length() - 1
                add = lam[level:level + 1] * sums[(lo_c, n // 2)]
                walk(lo_c, n // 2, base)
                walk(lo_c + n // 2, n // 2, add if base is None else base + add)

            walk(0, blocks, None)

    def lam_at(level, quarter):
        return lam_ref[level:level + 1, pl.ds(pl.multiple_of(quarter * qw, qw), qw)]

    def bit(b):
        return (s >> b & 1).astype(F32)

    c0 = s_send(0, tb, rsib, s ^ 1)
    w_send(a_pos < A - 1, s, True, blk(clamp(a_pos + 1, A), b_pos, core), wa.at[0, a_pos])
    w_send(a_pos > 0, s, True, blk(clamp(a_pos - 1, A), b_pos, core), wa.at[1, a_pos])
    row = lax.broadcasted_iota(jnp.int32, (BLOCK, BLOCK), 0)
    col = lax.broadcasted_iota(jnp.int32, (BLOCK, BLOCK), 1)
    for c in range(blocks):
        r = pl.ds(c * BLOCK, BLOCK)
        scores = dot(q_ref[r, :], k_ref[r, :], ((1,), (1,)))
        gsc[c] = jnp.where(row >= col, scores, 0.0).astype(BF16)
    c0.wait()
    first = 2 * core
    for i in range(2):
        t = tot[first + i] + rsib[first + i].astype(F32)
        half_f[i] = t
        half_b[i] = t.astype(BF16)
    c1 = s_send(1, half_b, r1, s ^ 2)
    across_b(0, True)
    send_core(True, a_pos, b_pos, True)
    cut = [tiles * i // (nbits - 1) for i in range(nbits)]
    local_tiles(cut[0], cut[1])
    c1.wait()
    mine = s >> 1 & 1
    qf[...] = half_f[mine] + r1[mine].astype(F32)
    for i in range(2):
        half_f[i] = bit(1) * lam_at(levels + 2, first + i) * r1[i].astype(F32)
    for b in range(2, nbits):
        qb[b - 2] = qf[...].astype(BF16)
        cb = s_send(b, qb.at[b - 2], rq.at[b - 2], s ^ (1 << b))
        local_tiles(cut[b - 1], cut[b])
        if b == nbits - 1:
            step_a(1)
        cb.wait()
        got = rq[b - 2].astype(F32)
        half_f[mine] += bit(b) * lam_at(levels + 1 + b, first + mine) * got
        contrib = bit(b) * lam_at(levels + 1 + b, first + mine) * got
        if b == 2:
            xs[1] = contrib
        else:
            xs[1] += contrib
        qf[...] += got
    qb[nbits - 2] = xs[1].astype(BF16)
    cx = s_send(nbits, qb.at[nbits - 2], xr, s ^ 2)
    across_b(1, True)
    cx.wait()
    half_f[1 - mine] += xr[...].astype(F32)
    hs[...] = half_f[...].astype(BF16)
    ch = s_send(nbits + 1, hs, hr, s ^ 1)
    ch.wait()
    other = 2 - first
    for i in range(2):
        acr[first + i] = (half_f[i] + bit(0) * lam_at(levels + 1, first + i) * rsib[first + i].astype(F32)).astype(BF16)
        acr[other + i] = (
            hr[i].astype(F32) + bit(0) * lam_at(levels + 1, other + i) * rsib[other + i].astype(F32)
        ).astype(BF16)
    gate_copy.wait()
    for j in range(2, min(3, A)):
        step_a(j)
        across_b(j, True)

    rt = 128
    row_tiles = tok // rt

    @pl.loop(0, row_tiles)
    def _(t):
        r = pl.ds(pl.multiple_of(t * rt, rt), rt)
        squares = jnp.zeros((rt, 1), F32)
        for i in range(4):
            at = slice(i * qw, (i + 1) * qw)
            mixed = loc[r, at] + dot(q_ref[r, :], acr[i], ((1,), (0,)))
            g = gate[r, at].astype(F32)
            gated = mixed * (g / (1.0 + jnp.exp(-g)))
            squares = squares + jnp.sum(gated * gated, axis=1, keepdims=True)
            gbuf[r, at] = (gated * gain_ref[:, at]).astype(BF16)
        wide = jnp.broadcast_to(squares, (rt, 128)).T
        ssq_own[:, r] = wide[0:8]

    sq = []
    for d in range(1, H):
        copy = remote(ssq_own, ssq_all.at[d], qs.at[d], qr.at[d], {"head": (h + d) % H})
        copy.start()
        sq.append(copy)

    own_copy.wait()

    nj, nw = psend.shape[1], psend.shape[3]
    per = nw // mr
    pt = 256
    ptiles = tok // pt

    def product(head, j, t):
        first_block = head * (nj * per) + j * per
        w = wbuf[pl.ds(first_block, per)].reshape(nw, cols)
        r = pl.ds(pl.multiple_of(t * pt, pt), pt)
        return dot(gbuf[r, :], w, ((1,), (1,))).astype(BF16), r

    def p_copy(d, j, t):
        r = pl.ds(pl.multiple_of(t * pt, pt), pt)
        return remote(
            psend.at[d, j, r], precv.at[d, j, r], ps.at[d, j, t], pr.at[d, j, t], {"head": (h + d) % H}
        )

    def far_steps():
        for j in range(3, A):
            step_a(j)
            across_b(j, True)
        for j in range(1, A):
            across_b(j, False)

    def send_chunk(d, j):
        @pl.loop(0, ptiles)
        def _(t):
            val, r = product((h + d) % H, j, t)
            psend[d, j, r] = val
            p_copy(d, j, t).start()

    def own_chunk(j):
        @pl.loop(0, ptiles)
        def _(t):
            val, r = product(h, j, t)
            pown[j, r] = val

    paired = H == 2 and A == 4 and B == 2 and nj == 4

    def chunk_order(half):
        low = half * 2
        near = jnp.where(jnp.abs(low - a_pos) <= jnp.abs(low + 1 - a_pos), 0, 1)
        return [2 * near + b_pos, 2 * near + 1 - b_pos, 2 * (1 - near) + b_pos, 2 * (1 - near) + 1 - b_pos]

    arrivals = list(range(nj))
    if paired:
        order = chunk_order(1 - h)
        arrivals = chunk_order(h)
        for i, j in enumerate(order):
            if i == 2:
                far_steps()
            ab = (1 - h) * 2 + j // 2
            finish_own(ab) if i % 2 == 0 else finish_rest(ab)
            send_chunk(1, j)
        for i, j in enumerate(arrivals):
            ab = h * 2 + j // 2
            finish_own(ab) if i % 2 == 0 else finish_rest(ab)
            own_chunk(j)
    else:
        far_steps()
        for i in range(A):
            finish_own(i)
            finish_rest(i)
        for d in range(1, H):
            for j in range(nj):
                send_chunk(d, j)
        for j in range(nj):
            own_chunk(j)

    for copy in sq:
        copy.wait()

    @pl.loop(0, ptiles)
    def _(t):
        r = pl.ds(pl.multiple_of(t * pt, pt), pt)
        total = ssq_own[:, r]
        for d in range(1, H):
            total = total + ssq_all[d, :, r]
        wide = jnp.broadcast_to(total[0:1], (128, pt)).T
        loc[r, 0:128] = lax.rsqrt(wide / INNER + EPSILON)

    for j in arrivals:
        @pl.loop(0, ptiles)
        def _(t, j=j):
            r = pl.ds(pl.multiple_of(t * pt, pt), pt)
            acc = pown[j, r].astype(F32)
            for d in range(1, H):
                p_copy(d, j, t).wait_recv()
                acc = acc + precv[d, j, r].astype(F32)
            scale = loc[r, 0:128][:, 0:1]
            out_ref[r, pl.ds(pl.multiple_of(j * nw, nw), nw)] = (acc * scale).astype(BF16)

    for d in range(1, H):
        @pl.loop(0, nj * ptiles)
        def _(i):
            p_copy(d, i // ptiles, i % ptiles).wait_send()
    for cond, copy in pending:
        when(cond, lambda: copy.wait_send())


def body(query_rows, key_rows, value_rows, gate_rows, norm_gain, level_table, level_index, out_weight):
    S, H = lax.axis_size("seq"), lax.axis_size("head")
    tok, state = query_rows.shape
    cols = value_rows.shape[1]
    mr = out_weight.shape[0]
    head_width = cols // level_index.shape[0]
    nlev = level_index.shape[1]
    blocks = tok // BLOCK
    nbits = S.bit_length() - 1
    choose = (level_index[:, :, None] == jnp.arange(level_table.shape[0], dtype=jnp.int32)).astype(F32)
    picked = jnp.sum(choose * level_table, axis=2)
    tiers = jnp.arange(nlev)
    bucket_sizes = BLOCK * jnp.exp2(jnp.maximum(tiers - 1, 0).astype(F32))
    weights = picked / jnp.sqrt(bucket_sizes)
    lam = jnp.repeat(weights, head_width, axis=0).T
    model_here = mr * S // H
    nw = min(256, model_here)
    nj = model_here // nw
    qw = cols // 4
    A = min(4, S // 2)
    B = S // (2 * A)
    ptiles = tok // 256
    vm = pl.BlockSpec(memory_space=pltpu.VMEM)
    hbm = pl.BlockSpec(memory_space=pl.ANY)
    dma = pltpu.SemaphoreType.DMA
    return pl.pallas_call(
        functools.partial(kernel, S, H),
        out_shape=jax.ShapeDtypeStruct((tok, model_here), BF16),
        in_specs=[vm, vm, vm, hbm, vm, vm, hbm],
        out_specs=vm,
        scratch_shapes=[
            pltpu.VMEM((tok, cols), BF16),
            pltpu.VMEM((S, mr, cols), BF16),
            pltpu.VMEM((tok, cols), F32),
            pltpu.VMEM((tok, cols), BF16),
            pltpu.VMEM((blocks, BLOCK, BLOCK), BF16),
            pltpu.VMEM((4, state, qw), F32),
            pltpu.VMEM((4, state, qw), BF16),
            pltpu.VMEM((4, state, qw), BF16),
            pltpu.VMEM((2, state, qw), F32),
            pltpu.VMEM((2, state, qw), BF16),
            pltpu.VMEM((2, state, qw), BF16),
            pltpu.VMEM((state, qw), F32),
            pltpu.VMEM((nbits, state, qw), BF16),
            pltpu.VMEM((nbits, state, qw), BF16),
            pltpu.VMEM((2, state, qw), F32),
            pltpu.VMEM((state, qw), BF16),
            pltpu.VMEM((2, state, qw), BF16),
            pltpu.VMEM((2, state, qw), BF16),
            pltpu.VMEM((4, state, qw), BF16),
            pltpu.VMEM((8, tok), F32),
            pltpu.VMEM((H, 8, tok), F32),
            pltpu.VMEM((H, nj, tok, nw), BF16),
            pltpu.VMEM((H, nj, tok, nw), BF16),
            pltpu.VMEM((nj, tok, nw), BF16),
            dma((2,)),
            dma((nbits + 2,)),
            dma((nbits + 2,)),
            dma((S,)),
            dma((2, A)),
            dma((2, A * B)),
            dma((A * B,)),
            dma((H,)),
            dma((H,)),
            dma((H, nj, ptiles)),
            dma((H, nj, ptiles)),
        ],
        compiler_params=pltpu.CompilerParams(
            collective_id=0, has_side_effects=True, vmem_limit_bytes=66 * 2**20 - 3 * 2**20
        ),
    )(query_rows, key_rows, value_rows, gate_rows, norm_gain.reshape(1, cols), lam, out_weight)


def solution(mesh):
    in_specs = (
        P("seq", None),
        P("seq", None),
        P("seq", "head"),
        P("seq", "head"),
        P("head"),
        P(),
        P("head", None),
        P("seq", "head"),
    )
    return jax.shard_map(body, mesh=mesh, in_specs=in_specs, out_specs=P("seq", "head"), check_vma=False)
```

```python
import functools

import jax
import jax.numpy as jnp
from jax import lax
from jax.experimental import pallas as pl
from jax.experimental.pallas import tpu as pltpu
from jax.sharding import PartitionSpec as P

BLOCK = 64
INNER = 4096
EPSILON = 1e-05
F32 = jnp.float32
BF16 = jnp.bfloat16
MESH = pl.DeviceIdType.MESH


def dot(a, b, dims):
    return lax.dot_general(a, b, (dims, ((), ())), preferred_element_type=F32)


def kernel(
    S, H, q_ref, k_ref, v_ref, gate_hbm, gain_ref, lam_ref, w_hbm, out_ref,
    gate, wbuf, loc, gbuf, gsc, tot, tb, rsib, half_f, half_b, r1, qf, qb, rq, xs, xr, hs, hr, acr,
    ssq_own, ssq_all, psend, precv, pown,
    lsem, ssem, rsem, wr, wa, wb, wc, qs, qr, ps, pr,
):
    tok, state = q_ref.shape
    cols = v_ref.shape[1]
    mr = w_hbm.shape[0]
    blocks = tok // BLOCK
    levels = blocks.bit_length() - 1
    nbits = S.bit_length() - 1
    qw = cols // 4
    A = min(4, S // 2)
    B = S // (2 * A)
    s = lax.axis_index("seq")
    h = lax.axis_index("head")
    core, b_pos, a_pos = s % 2, (s // 2) % B, s // (2 * B)

    barrier = pltpu.get_barrier_semaphore()
    for d in range(1, S):
        pl.semaphore_signal(barrier, inc=1, device_id={"seq": (s + d) % S}, device_id_type=MESH)
    for d in range(1, H):
        pl.semaphore_signal(barrier, inc=1, device_id={"head": (h + d) % H}, device_id_type=MESH)
    gate_copy = pltpu.make_async_copy(gate_hbm, gate, lsem.at[0])
    gate_copy.start()
    own_copy = pltpu.make_async_copy(w_hbm, wbuf.at[s], lsem.at[1])
    own_copy.start()

    for i in range(4):
        t = dot(k_ref[...], v_ref[:, i * qw:(i + 1) * qw], ((0,), (0,)))
        tot[i] = t
        tb[i] = t.astype(BF16)
    pl.semaphore_wait(barrier, S + H - 2)

    pending = []

    def remote(src, dst, send, recv, target):
        return pltpu.make_async_remote_copy(
            src_ref=src, dst_ref=dst, send_sem=send, recv_sem=recv,
            device_id=target, device_id_type=MESH,
        )

    def when(cond, fn):
        if cond is True:
            fn()
        else:
            pl.when(cond)(fn)

    def w_send(cond, block, own, target, sem):
        copy = remote(w_hbm if own else wbuf.at[block], wbuf.at[block], sem, wr.at[block], {"seq": target})
        when(cond, lambda: copy.start())
        pending.append((cond, copy))

    def w_wait(cond, block, sem):
        copy = remote(wbuf.at[block], wbuf.at[block], sem, wr.at[block], {"seq": s ^ 1})
        when(cond, lambda: copy.wait_recv())

    def both(x, y):
        return y if x is True else (x if y is True else jnp.logical_and(x, y))

    def blk(a, b, c):
        return (a * B + b) * 2 + c

    def clamp(x, n):
        return jnp.minimum(jnp.maximum(x, 0), n - 1)

    def send_b(cond, ab, own):
        block = blk(ab, b_pos, core)
        if B > 1:
            w_send(both(cond, b_pos < B - 1), block, own, blk(a_pos, clamp(b_pos + 1, B), core), wb.at[0, ab * B + b_pos])
            w_send(both(cond, b_pos > 0), block, own, blk(a_pos, clamp(b_pos - 1, B), core), wb.at[1, ab * B + b_pos])

    def send_core(cond, ab, bb, own):
        w_send(cond, blk(ab, bb, core), own, s ^ 1, wc.at[ab * B + bb])

    def urgent(ab):
        return ab * H // A != h

    def source_a(j, sign):
        ab = a_pos - sign * j
        cond = ab >= 0 if sign == 1 else ab <= A - 1
        return cond, clamp(ab, A)

    def across_b(j, first):
        if j == 0:
            send_b(True, a_pos, True)
            return
        for sign in (1, -1):
            cond, ab = source_a(j, sign)
            send_b(both(cond, urgent(ab) if first else jnp.logical_not(urgent(ab))), ab, False)

    def step_a(j):
        for sign in (1, -1):
            cond, ab = source_a(j, sign)
            block = blk(ab, b_pos, core)
            w_wait(cond, block, wc.at[0])
            onward = a_pos < A - 1 if sign == 1 else a_pos > 0
            nxt = clamp(a_pos + sign, A)
            w_send(both(cond, onward), block, False, blk(nxt, b_pos, core), wa.at[(1 - sign) // 2, ab])
            send_core(cond, ab, b_pos, False)

    def finish_own(ab):
        w_wait(True, blk(ab, b_pos, 1 - core), wc.at[0])

    def finish_rest(ab):
        for j in range(1, B):
            for sign in (1, -1):
                bb = b_pos - sign * j
                cond = bb >= 0 if sign == 1 else bb <= B - 1
                bb = clamp(bb, B)
                onward = both(cond, b_pos < B - 1 if sign == 1 else b_pos > 0)
                block = blk(ab, bb, core)
                w_wait(cond, block, wc.at[0])
                if B > 2:
                    w_send(onward, block, False, blk(a_pos, clamp(b_pos + sign, B), core), wb.at[(1 - sign) // 2, ab * B + bb])
                send_core(cond, ab, bb, False)
        for j in range(1, B):
            w_wait(True, blk(ab, lax.rem(b_pos + j, B), 1 - core), wc.at[0])

    def s_send(i, src, dst, target):
        copy = remote(src, dst, ssem.at[i], rsem.at[i], {"seq": target})
        copy.start()
        return copy

    tw = min(256, cols)
    tiles = cols // tw

    def local_tiles(lo, hi):
        @pl.loop(lo, hi)
        def _(ct):
            at = pl.ds(pl.multiple_of(ct * tw, tw), tw)
            lam = lam_ref[:, at]

            def vals(c):
                return v_ref[pl.ds(c * BLOCK, BLOCK), at]

            def total(lo_c, n):
                if n == 1:
                    r = pl.ds(lo_c * BLOCK, BLOCK)
                    return dot(k_ref[r, :], vals(lo_c), ((0,), (0,)))
                return sums[(lo_c, n // 2)] + sums[(lo_c + n // 2, n // 2)]

            sums = {}
            n = 1
            while n < blocks:
                for lo_c in range(0, blocks, n):
                    sums[(lo_c, n)] = total(lo_c, n)
                n *= 2

            def walk(lo_c, n, base):
                if n == 1:
                    r = pl.ds(lo_c * BLOCK, BLOCK)
                    m = lam[0:1] * dot(gsc[lo_c], vals(lo_c), ((1,), (0,)))
                    if base is not None:
                        m = m + dot(q_ref[r, :], base.astype(BF16), ((1,), (0,)))
                    loc[r, at] = m
                    return
                level = n.bit_length() - 1
                add = lam[level:level + 1] * sums[(lo_c, n // 2)]
                walk(lo_c, n // 2, base)
                walk(lo_c + n // 2, n // 2, add if base is None else base + add)

            walk(0, blocks, None)

    def lam_at(level, quarter):
        return lam_ref[level:level + 1, pl.ds(pl.multiple_of(quarter * qw, qw), qw)]

    def bit(b):
        return (s >> b & 1).astype(F32)

    c0 = s_send(0, tb, rsib, s ^ 1)
    w_send(a_pos < A - 1, s, True, blk(clamp(a_pos + 1, A), b_pos, core), wa.at[0, a_pos])
    w_send(a_pos > 0, s, True, blk(clamp(a_pos - 1, A), b_pos, core), wa.at[1, a_pos])
    row = lax.broadcasted_iota(jnp.int32, (BLOCK, BLOCK), 0)
    col = lax.broadcasted_iota(jnp.int32, (BLOCK, BLOCK), 1)
    for c in range(blocks):
        r = pl.ds(c * BLOCK, BLOCK)
        scores = dot(q_ref[r, :], k_ref[r, :], ((1,), (1,)))
        gsc[c] = jnp.where(row >= col, scores, 0.0).astype(BF16)
    c0.wait()
    first = 2 * core
    for i in range(2):
        t = tot[first + i] + rsib[first + i].astype(F32)
        half_f[i] = t
        half_b[i] = t.astype(BF16)
    c1 = s_send(1, half_b, r1, s ^ 2)
    across_b(0, True)
    send_core(True, a_pos, b_pos, True)
    cut = [tiles * i // (nbits - 1) for i in range(nbits)]
    local_tiles(cut[0], cut[1])
    c1.wait()
    mine = s >> 1 & 1
    qf[...] = half_f[mine] + r1[mine].astype(F32)
    for i in range(2):
        half_f[i] = bit(1) * lam_at(levels + 2, first + i) * r1[i].astype(F32)
    for b in range(2, nbits):
        qb[b - 2] = qf[...].astype(BF16)
        cb = s_send(b, qb.at[b - 2], rq.at[b - 2], s ^ (1 << b))
        local_tiles(cut[b - 1], cut[b])
        if b == nbits - 1:
            step_a(1)
        cb.wait()
        got = rq[b - 2].astype(F32)
        half_f[mine] += bit(b) * lam_at(levels + 1 + b, first + mine) * got
        contrib = bit(b) * lam_at(levels + 1 + b, first + mine) * got
        if b == 2:
            xs[1] = contrib
        else:
            xs[1] += contrib
        qf[...] += got
    qb[nbits - 2] = xs[1].astype(BF16)
    cx = s_send(nbits, qb.at[nbits - 2], xr, s ^ 2)
    across_b(1, True)
    cx.wait()
    half_f[1 - mine] += xr[...].astype(F32)
    hs[...] = half_f[...].astype(BF16)
    ch = s_send(nbits + 1, hs, hr, s ^ 1)
    ch.wait()
    other = 2 - first
    for i in range(2):
        acr[first + i] = (half_f[i] + bit(0) * lam_at(levels + 1, first + i) * rsib[first + i].astype(F32)).astype(BF16)
        acr[other + i] = (
            hr[i].astype(F32) + bit(0) * lam_at(levels + 1, other + i) * rsib[other + i].astype(F32)
        ).astype(BF16)
    gate_copy.wait()
    for j in range(2, min(3, A)):
        step_a(j)
        across_b(j, True)

    rt = 128
    row_tiles = tok // rt

    @pl.loop(0, row_tiles)
    def _(t):
        r = pl.ds(pl.multiple_of(t * rt, rt), rt)
        squares = jnp.zeros((rt, 1), F32)
        for i in range(4):
            at = slice(i * qw, (i + 1) * qw)
            mixed = loc[r, at] + dot(q_ref[r, :], acr[i], ((1,), (0,)))
            g = gate[r, at].astype(F32)
            gated = mixed * (g / (1.0 + jnp.exp(-g)))
            squares = squares + jnp.sum(gated * gated, axis=1, keepdims=True)
            gbuf[r, at] = (gated * gain_ref[:, at]).astype(BF16)
        wide = jnp.broadcast_to(squares, (rt, 128)).T
        ssq_own[:, r] = wide[0:8]

    sq = []
    for d in range(1, H):
        copy = remote(ssq_own, ssq_all.at[d], qs.at[d], qr.at[d], {"head": (h + d) % H})
        copy.start()
        sq.append(copy)

    own_copy.wait()

    nj, nw = psend.shape[1], psend.shape[3]
    per = nw // mr
    pt = 256
    ptiles = tok // pt

    def product(head, j, t):
        first_block = head * (nj * per) + j * per
        w = wbuf[pl.ds(first_block, per)].reshape(nw, cols)
        r = pl.ds(pl.multiple_of(t * pt, pt), pt)
        return dot(gbuf[r, :], w, ((1,), (1,))).astype(BF16), r

    def p_copy(d, j, t):
        r = pl.ds(pl.multiple_of(t * pt, pt), pt)
        return remote(
            psend.at[d, j, r], precv.at[d, j, r], ps.at[d, j, t], pr.at[d, j, t], {"head": (h + d) % H}
        )

    def far_steps():
        for j in range(3, A):
            step_a(j)
            across_b(j, True)
        for j in range(1, A):
            across_b(j, False)

    def send_chunk(d, j):
        @pl.loop(0, ptiles)
        def _(t):
            val, r = product((h + d) % H, j, t)
            psend[d, j, r] = val
            p_copy(d, j, t).start()

    def own_chunk(j):
        @pl.loop(0, ptiles)
        def _(t):
            val, r = product(h, j, t)
            pown[j, r] = val

    paired = H == 2 and A == 4 and B == 2 and nj == 4

    def chunk_order(half):
        low = half * 2
        near = jnp.where(jnp.abs(low - a_pos) <= jnp.abs(low + 1 - a_pos), 0, 1)
        return [2 * near + b_pos, 2 * near + 1 - b_pos, 2 * (1 - near) + b_pos, 2 * (1 - near) + 1 - b_pos]

    arrivals = list(range(nj))
    if paired:
        order = chunk_order(1 - h)
        arrivals = chunk_order(h)
        for i, j in enumerate(order):
            if i == 1:
                far_steps()
            ab = (1 - h) * 2 + j // 2
            finish_own(ab) if i % 2 == 0 else finish_rest(ab)
            send_chunk(1, j)
        for i, j in enumerate(arrivals):
            ab = h * 2 + j // 2
            finish_own(ab) if i % 2 == 0 else finish_rest(ab)
            own_chunk(j)
    else:
        far_steps()
        for i in range(A):
            finish_own(i)
            finish_rest(i)
        for d in range(1, H):
            for j in range(nj):
                send_chunk(d, j)
        for j in range(nj):
            own_chunk(j)

    for copy in sq:
        copy.wait()

    @pl.loop(0, ptiles)
    def _(t):
        r = pl.ds(pl.multiple_of(t * pt, pt), pt)
        total = ssq_own[:, r]
        for d in range(1, H):
            total = total + ssq_all[d, :, r]
        wide = jnp.broadcast_to(total[0:1], (128, pt)).T
        loc[r, 0:128] = lax.rsqrt(wide / INNER + EPSILON)

    for j in arrivals:
        @pl.loop(0, ptiles)
        def _(t, j=j):
            r = pl.ds(pl.multiple_of(t * pt, pt), pt)
            acc = pown[j, r].astype(F32)
            for d in range(1, H):
                p_copy(d, j, t).wait_recv()
                acc = acc + precv[d, j, r].astype(F32)
            scale = loc[r, 0:128][:, 0:1]
            out_ref[r, pl.ds(pl.multiple_of(j * nw, nw), nw)] = (acc * scale).astype(BF16)

    for d in range(1, H):
        @pl.loop(0, nj * ptiles)
        def _(i):
            p_copy(d, i // ptiles, i % ptiles).wait_send()
    for cond, copy in pending:
        when(cond, lambda: copy.wait_send())


def body(query_rows, key_rows, value_rows, gate_rows, norm_gain, level_table, level_index, out_weight):
    S, H = lax.axis_size("seq"), lax.axis_size("head")
    tok, state = query_rows.shape
    cols = value_rows.shape[1]
    mr = out_weight.shape[0]
    head_width = cols // level_index.shape[0]
    nlev = level_index.shape[1]
    blocks = tok // BLOCK
    nbits = S.bit_length() - 1
    choose = (level_index[:, :, None] == jnp.arange(level_table.shape[0], dtype=jnp.int32)).astype(F32)
    picked = jnp.sum(choose * level_table, axis=2)
    tiers = jnp.arange(nlev)
    bucket_sizes = BLOCK * jnp.exp2(jnp.maximum(tiers - 1, 0).astype(F32))
    weights = picked / jnp.sqrt(bucket_sizes)
    lam = jnp.repeat(weights, head_width, axis=0).T
    model_here = mr * S // H
    nw = min(256, model_here)
    nj = model_here // nw
    qw = cols // 4
    A = min(4, S // 2)
    B = S // (2 * A)
    ptiles = tok // 256
    vm = pl.BlockSpec(memory_space=pltpu.VMEM)
    hbm = pl.BlockSpec(memory_space=pl.ANY)
    dma = pltpu.SemaphoreType.DMA
    return pl.pallas_call(
        functools.partial(kernel, S, H),
        out_shape=jax.ShapeDtypeStruct((tok, model_here), BF16),
        in_specs=[vm, vm, vm, hbm, vm, vm, hbm],
        out_specs=vm,
        scratch_shapes=[
            pltpu.VMEM((tok, cols), BF16),
            pltpu.VMEM((S, mr, cols), BF16),
            pltpu.VMEM((tok, cols), F32),
            pltpu.VMEM((tok, cols), BF16),
            pltpu.VMEM((blocks, BLOCK, BLOCK), BF16),
            pltpu.VMEM((4, state, qw), F32),
            pltpu.VMEM((4, state, qw), BF16),
            pltpu.VMEM((4, state, qw), BF16),
            pltpu.VMEM((2, state, qw), F32),
            pltpu.VMEM((2, state, qw), BF16),
            pltpu.VMEM((2, state, qw), BF16),
            pltpu.VMEM((state, qw), F32),
            pltpu.VMEM((nbits, state, qw), BF16),
            pltpu.VMEM((nbits, state, qw), BF16),
            pltpu.VMEM((2, state, qw), F32),
            pltpu.VMEM((state, qw), BF16),
            pltpu.VMEM((2, state, qw), BF16),
            pltpu.VMEM((2, state, qw), BF16),
            pltpu.VMEM((4, state, qw), BF16),
            pltpu.VMEM((8, tok), F32),
            pltpu.VMEM((H, 8, tok), F32),
            pltpu.VMEM((H, nj, tok, nw), BF16),
            pltpu.VMEM((H, nj, tok, nw), BF16),
            pltpu.VMEM((nj, tok, nw), BF16),
            dma((2,)),
            dma((nbits + 2,)),
            dma((nbits + 2,)),
            dma((S,)),
            dma((2, A)),
            dma((2, A * B)),
            dma((A * B,)),
            dma((H,)),
            dma((H,)),
            dma((H, nj, ptiles)),
            dma((H, nj, ptiles)),
        ],
        compiler_params=pltpu.CompilerParams(
            collective_id=0, has_side_effects=True, vmem_limit_bytes=66 * 2**20 - 3 * 2**20
        ),
    )(query_rows, key_rows, value_rows, gate_rows, norm_gain.reshape(1, cols), lam, out_weight)


def solution(mesh):
    in_specs = (
        P("seq", None),
        P("seq", None),
        P("seq", "head"),
        P("seq", "head"),
        P("head"),
        P(),
        P("head", None),
        P("seq", "head"),
    )
    return jax.shard_map(body, mesh=mesh, in_specs=in_specs, out_specs=P("seq", "head"), check_vma=False)
```
